32 devices in a mesh: rows: 16 (over z, y, x), genes: 2 (over core).
Axes of the slice: x: 2, y: 2, z: 4, core: 2. Of those that a mesh axis runs over, the one named last changes fastest.
Arguments:
- tokens: bfloat16 [16, 2048, 768], P('rows', 'genes'), may hold values from -6 to 6
- segment_ids: int32 [16, 2048], P('rows'), may hold values from 0 to 7, never falling along the last dimension, each value on 1 to 512 neighbouring positions
- cotangent: bfloat16 [16, 2048, 768], P('rows', 'genes'), may hold values from -6 to 6
- matrices: float32 [3, 768, 3072], P(None, ('rows', 'genes')), may hold values from -0.57735027 to 0.57735027
- vectors: float32 [12, 768], P(None, ('rows', 'genes')), may hold values from -1.2 to 1.8
- mat_first: float32 [3, 768, 3072], P(None, ('rows', 'genes')), may hold values from -135.7645 to 135.7645
- mat_second: float32 [3, 768, 3072], P(None, ('rows', 'genes')), may hold values from 327.68 to 32768
- vec_first: float32 [12, 768], P(None, ('rows', 'genes')), may hold values from -135.7645 to 135.7645
- vec_second: float32 [12, 768], P(None, ('rows', 'genes')), may hold values from 8192 to 32768
Outputs:
- layer_out: bfloat16 [16, 2048, 768], P('rows', 'genes')
- tokens_grad: float32 [16, 2048, 768], P('rows', 'genes')
- matrices_new: float32 [3, 768, 3072], P(None, ('rows', 'genes'))
- matrices_first: float32 [3, 768, 3072], P(None, ('rows', 'genes'))
- matrices_second: float32 [3, 768, 3072], P(None, ('rows', 'genes'))
- vectors_new: float32 [12, 768], P(None, ('rows', 'genes'))
- vectors_first: float32 [12, 768], P(None, ('rows', 'genes'))
- vectors_second: float32 [12, 768], P(None, ('rows', 'genes'))
The draws below stay inside these ranges and needn't reach their ends.
Inputs may be any that keep to these rules, and one draw needn't show every extreme that they name: `segment_ids`: within a row the ids never fall; each cell holds 1 to 512 genes, one cell of each row exactly 512.
All inputs are finite; a program needn't handle non-finite values.
Results may differ from the reference program's by a relative error of at most 0.011.
Values may be sent and summed in bfloat16 or wider, within the bound.
No kernel may reach another device: no remote copies, remote signals or barrier semaphores. Data moves between devices by JAX's collectives and lax.ppermute only.
A program may use at most 256 MiB of HBM per device.

```python
import math
import jax
import jax.numpy as jnp
import numpy as np
from jax import lax

D = 768
HEADS = 12
HD = 64
FF = 3072
L = 2048
CELLS = 8
CELL_MAX = 512
STEP = 10
ROWS = 16


def matrix_factor():
    shape = (3, D, FF)
    slab = lax.broadcasted_iota(jnp.int32, shape, 0)
    column = lax.broadcasted_iota(jnp.int32, shape, 2)
    return (slab, column)


def matrix_gradient_size():
    slab, column = matrix_factor()
    factor = jnp.where(slab == 1, 0.2, 0.5)
    inner = jnp.where(column < 2 * D, 0.1, jnp.where(column < 3 * D, 0.3, 0.2))
    factor = jnp.where(slab == 0, inner, factor)
    return factor * (ROWS * L) ** 0.5


def draw_matrices(key, part):
    shape = (3, D, FF)
    normal = jax.random.truncated_normal(jax.random.fold_in(key, 11), -4.0, 4.0, shape, jnp.float32)
    slab, column = matrix_factor()
    factor = jnp.where(slab == 2, FF ** (-0.5), D ** (-0.5))
    factor = jnp.where((slab == 0) & (column >= 3 * D), 4.0 * D ** (-0.5), factor)
    return normal * factor


def draw_vectors(key, part):
    shape = (12, D)
    normal = jax.random.truncated_normal(jax.random.fold_in(key, 31), -3.0, 3.0, shape, jnp.float32)
    row_index = lax.broadcasted_iota(jnp.int32, shape, 0)
    gain_rows = (row_index == 0) | (row_index == 5)
    return jnp.where(gain_rows, 1.0 + 0.2 * normal, 0.3 * normal)


def signed_first(key, shape, size_table):
    magnitude = jax.random.uniform(jax.random.fold_in(key, 41), shape, jnp.float32, 0.5, 1.5)
    signs = jnp.where(jax.random.bernoulli(jax.random.fold_in(key, 42), 0.5, shape), 1.0, -1.0)
    return size_table * magnitude * signs


def positive_second(key, shape, size_table):
    factor = jax.random.uniform(jax.random.fold_in(key, 51), shape, jnp.float32, 1.0, 4.0)
    return size_table * size_table * factor


def draw_mat_first(key, part):
    return signed_first(jax.random.fold_in(key, 61), (3, D, FF), matrix_gradient_size())


def draw_mat_second(key, part):
    return positive_second(jax.random.fold_in(key, 62), (3, D, FF), matrix_gradient_size())


def draw_vec_first(key, part):
    size_table = jnp.full((12, D), 0.5 * (ROWS * L) ** 0.5, jnp.float32)
    return signed_first(jax.random.fold_in(key, 63), (12, D), size_table)


def draw_vec_second(key, part):
    size_table = jnp.full((12, D), 0.5 * (ROWS * L) ** 0.5, jnp.float32)
    return positive_second(jax.random.fold_in(key, 64), (12, D), size_table)


def shard_levels(stream_key, dims, pieces, low, high):
    def one(dim, shards_of):
        steps = jax.random.uniform(jax.random.fold_in(jax.random.fold_in(stream_key, 6), dim), (shards_of,), jnp.float32, low / len(pieces), high / len(pieces))
        return jnp.repeat(jnp.exp(steps), dims[dim] // shards_of).reshape((-1,) + (1,) * (len(dims) - dim - 1))

    gain = one(*pieces[0])
    for cut in pieces[1:]:
        gain = gain * one(*cut)
    return gain


def length_profile(count, total, bound, lean):
    portions = [(1 << 20) // math.isqrt(rank ** lean) + 1 for rank in range(2, count + 1)]
    rest, holding = total - bound - (count - 1), [1] * (count - 1)
    while rest > 0:
        free = [i for i in range(count - 1) if holding[i] < bound]
        mass, remaining = sum([portions[i] for i in free]), rest
        for i in free:
            extra = min(bound - holding[i], max(1, remaining * portions[i] // mass), rest)
            holding[i] = holding[i] + extra
            rest = rest - extra
    return np.array([bound] + holding)


def ragged(key, amount, total, reach, skew):
    if amount == 2:
        one = jax.random.randint(key, (), max(1, total - reach), min(reach, total - 1) + 1)
        return jnp.stack([one, total - one])
    sizes = jnp.asarray(length_profile(amount, total, reach, skew), jnp.int32)
    pairs = (amount - 1) // 2
    donor, receiver = sizes[1:1 + 2 * pairs:2], sizes[2:2 + 2 * pairs:2]
    margin = jnp.minimum(donor - 1, reach - receiver)
    moved = jax.random.randint(jax.random.fold_in(key, 1), (pairs,), 0, 1 << 20) % (margin + 1)
    sizes = sizes.at[1:1 + 2 * pairs:2].set(donor - moved).at[2:2 + 2 * pairs:2].set(receiver + moved)
    return sizes[jax.random.permutation(jax.random.fold_in(key, 2), amount)]


def normal_values(key, dims, width, bound, pieces=(), kind=jnp.bfloat16):
    values = width * jax.random.normal(key, dims, jnp.float32)
    if pieces:
        values = values * shard_levels(key, dims, pieces, -0.22, 0.18)
    return jnp.clip(values, -bound, bound).astype(kind)


def setup_inputs(seed: int = 0) -> dict:
    splits = jax.random.split(jax.random.key(seed), 10)
    tokens = normal_values(splits[0], (ROWS, L, D), 1.0, 6.0, ((0, 16), (1, 2)))
    segment_ids = jax.vmap(lambda own: jnp.searchsorted(jnp.cumsum(ragged(own, CELLS, L, CELL_MAX, 2)), jnp.arange(L), side="right"))(jax.random.split(splits[1], ROWS)).reshape((ROWS, L)).astype(jnp.int32)
    cotangent = normal_values(splits[2], (ROWS, L, D), 1.0, 6.0, ((0, 16), (1, 2)))
    matrices = draw_matrices(jax.random.fold_in(splits[9], 71), 0)
    vectors = draw_vectors(jax.random.fold_in(splits[9], 71), 0)
    mat_first = draw_mat_first(jax.random.fold_in(splits[9], 71), 0)
    mat_second = draw_mat_second(jax.random.fold_in(splits[9], 71), 0)
    vec_first = draw_vec_first(jax.random.fold_in(splits[9], 71), 0)
    vec_second = draw_vec_second(jax.random.fold_in(splits[9], 71), 0)
    return dict(tokens=tokens, segment_ids=segment_ids, cotangent=cotangent, matrices=matrices, vectors=vectors, mat_first=mat_first, mat_second=mat_second, vec_first=vec_first, vec_second=vec_second)


@jax.custom_vjp
def low(v):
    return lax.optimization_barrier(v.astype(jnp.bfloat16)).astype(jnp.float32)

@jax.custom_vjp
def low_back(v):
    return v

def low_keep(v):
    return (low(v), None)

def low_pass(kept, grad):
    return (grad,)

def back_keep(v):
    return (v, None)

def back_low(kept, grad):
    return (low(grad),)
low.defvjp(low_keep, low_pass)
low_back.defvjp(back_keep, back_low)
BETA_FIRST = 0.5
BETA_SECOND = 0.5
ADAM_EPS = 1e-08
MATRIX_RATE = 0.05
VECTOR_RATE = 0.3
MATRIX_DECAY = 0.01
NORM_EPS = 1e-05
HIGHEST = lax.Precision.HIGHEST

def norm_rows(values, gain_row, shift_row):
    centre = values - lax.optimization_barrier(jnp.mean(values, axis=-1, keepdims=True))
    spread = lax.optimization_barrier(jnp.mean(centre * centre, axis=-1, keepdims=True))
    return centre * lax.rsqrt(spread + NORM_EPS) * gain_row + shift_row

def product(former, latter):
    return jnp.dot(former, latter, precision=HIGHEST)

def attention_row(queries, key_rows, value_rows, segments):
    block_len = min(512, L)
    score_scale = HD ** (-0.5)

    def one_block(inputs):
        query_block, segment_block = inputs
        scores = jnp.einsum('qhd,khd->hqk', query_block, key_rows, precision=HIGHEST) * score_scale
        scores = low_back(scores)
        allowed = (segment_block[:, None] == segments[None, :])[None]
        scores = jnp.where(allowed, scores, -1e+30)
        largest = lax.optimization_barrier(jnp.max(scores, axis=-1, keepdims=True))
        weights = jnp.exp(scores - largest)
        probs_low = low(weights / lax.optimization_barrier(jnp.sum(weights, axis=-1, keepdims=True)))
        return jnp.einsum('hqk,khd->qhd', probs_low, value_rows, precision=HIGHEST)
    context = lax.map(jax.checkpoint(one_block), (queries.reshape(L // block_len, block_len, HEADS, HD), segments.reshape(L // block_len, block_len)))
    return context.reshape(L, HEADS * HD)

def forward_row(tokens_row, matrices, vectors, segments):
    normed = low(norm_rows(tokens_row, vectors[0], vectors[1]))
    projected = product(normed, matrices[0][:, :3 * D])
    queries = low(low_back(projected[:, :D] + vectors[2]))
    key_rows = low(low_back(projected[:, D:2 * D]))
    value_rows = low(low_back(projected[:, 2 * D:] + vectors[3]))
    head_shape = (L, HEADS, HD)
    context = attention_row(queries.reshape(head_shape), key_rows.reshape(head_shape), value_rows.reshape(head_shape), segments)
    context = low(low_back(context))
    branch = low_back(product(context, matrices[0][:, 3 * D:]) + vectors[4])
    middle = tokens_row + branch
    normed_two = low(norm_rows(middle, vectors[5], vectors[6]))
    pre_act = low_back(product(normed_two, matrices[1]) + vectors[7:11].reshape(FF))
    activated = low(jax.nn.gelu(pre_act, approximate=False))
    return middle + jnp.dot(activated, matrices[2].T, precision=HIGHEST) + vectors[11]

def adamw(master, gradient, first, second, rate, decay):
    first_new = BETA_FIRST * first + (1.0 - BETA_FIRST) * gradient
    second_new = BETA_SECOND * second + (1.0 - BETA_SECOND) * gradient * gradient
    first_hat = first_new / (1.0 - BETA_FIRST ** STEP)
    second_hat = second_new / (1.0 - BETA_SECOND ** STEP)
    master_new = master - rate * (first_hat / (jnp.sqrt(second_hat) + ADAM_EPS) + decay * master)
    return (master_new, first_new, second_new)

def reference(tokens, segment_ids, cotangent, matrices, vectors, mat_first, mat_second, vec_first, vec_second):
    matrix_low = matrices.astype(jnp.bfloat16).astype(jnp.float32)
    vector_low = vectors.astype(jnp.bfloat16).astype(jnp.float32)

    def row_step(carry, inputs):
        tokens_row, segment_row, cotangent_row = inputs

        def forward(row_in, matrix_in, vector_in):
            return forward_row(row_in, matrix_in, vector_in, segment_row)
        output, pullback = jax.vjp(forward, tokens_row.astype(jnp.float32), matrix_low, vector_low)
        grad_row, grad_matrix, grad_vector = pullback(cotangent_row.astype(jnp.float32))
        return ((carry[0] + grad_matrix, carry[1] + grad_vector), (output.astype(jnp.bfloat16), grad_row))
    start = (jnp.zeros(matrices.shape, jnp.float32), jnp.zeros(vectors.shape, jnp.float32))
    (grad_matrix, grad_vector), (layer_out, tokens_grad) = lax.scan(row_step, start, (tokens, segment_ids, cotangent))
    matrices_new, matrices_first, matrices_second = adamw(matrices, grad_matrix, mat_first, mat_second, MATRIX_RATE, MATRIX_DECAY)
    vectors_new, vectors_first, vectors_second = adamw(vectors, grad_vector, vec_first, vec_second, VECTOR_RATE, 0.0)
    return (layer_out, tokens_grad, matrices_new, matrices_first, matrices_second, vectors_new, vectors_first, vectors_second)
```

```python
import jax
import jax.numpy as jnp
from jax import lax
from jax.experimental import pallas as pl
from jax.experimental.pallas import tpu as pltpu
from jax.sharding import PartitionSpec as P

HD = 64
STEP = 10
CELL_MAX = 512

BETA_FIRST = 0.5
BETA_SECOND = 0.5
ADAM_EPS = 1e-08
MATRIX_RATE = 0.05
VECTOR_RATE = 0.3
MATRIX_DECAY = 0.01
NORM_EPS = 1e-05
SCORE_MASK = -1e30
PAIR = 2 * HD
QBLK = 256
KBLK = 256
VEC_COLS = 128

F32 = jnp.float32
BF16 = jnp.bfloat16


def contract_rows(former, latter):
    return lax.dot_general(
        former, latter, (((0,), (0,)), ((), ())), preferred_element_type=jnp.float32
    )


def contract_cols(former, latter):
    return lax.dot_general(
        former, latter, (((1,), (1,)), ((), ())), preferred_element_type=jnp.float32
    )


def matmul(former, latter):
    return lax.dot_general(
        former, latter, (((1,), (0,)), ((), ())), preferred_element_type=jnp.float32
    )


def norm_stats(values):
    centre = values - jnp.mean(values, axis=-1, keepdims=True)
    spread = jnp.mean(centre * centre, axis=-1, keepdims=True)
    factor = lax.rsqrt(spread + NORM_EPS)
    return centre * factor, factor


def norm_back(grad, hat, factor, gain):
    scaled = grad * gain
    mean_one = jnp.mean(scaled, axis=-1, keepdims=True)
    mean_two = jnp.mean(scaled * hat, axis=-1, keepdims=True)
    return factor * (scaled - mean_one - hat * mean_two)


def normal_parts(values):
    bell = jnp.exp(-0.5 * values * values)
    t = 1.0 / (1.0 + 0.3275911 * 0.7071067811865476 * jnp.abs(values))
    poly = t * (
        0.254829592
        + t * (-0.284496736 + t * (1.421413741 + t * (-1.453152027 + t * 1.061405429)))
    )
    tail = 0.5 * poly * bell
    return jnp.where(values < 0.0, tail, 1.0 - tail), 0.3989422804014327 * bell


def split_pair(block):
    lane = lax.broadcasted_iota(jnp.int32, block.shape, 1)
    zero = jnp.zeros_like(block)
    return jnp.concatenate(
        [jnp.where(lane < HD, block, zero), jnp.where(lane < HD, zero, block)], 0
    )


def tile_lanes(block, times):
    return jnp.concatenate([block] * times, 1)


def attn_forward_kernel(
    table, q_ref, k_ref, v_ref, kh_ref, vh_ref, segq_ref, segk_ref, ctx_ref, lse_ref, k_all, v_turn
):
    own = k_ref.shape[0]
    halo = kh_ref.shape[0]
    k_all[:own, :] = k_ref[...]
    k_all[own:, :] = kh_ref[...]
    for b in range(own // KBLK):
        v_turn[b] = v_ref[b * KBLK : (b + 1) * KBLK, :].T
    for b in range(halo // KBLK):
        v_turn[own // KBLK + b] = vh_ref[b * KBLK : (b + 1) * KBLK, :].T
    for i in range(own // QBLK):
        rows = slice(i * QBLK, (i + 1) * QBLK)
        queries = split_pair(q_ref[rows, :] * BF16(HD**-0.5))
        seg_q = tile_lanes(segq_ref[:, rows], 2)

        def step(j, carry):
            largest, total, acc_a, acc_b = carry
            b = table[i, j + 1]
            at = pl.ds(pl.multiple_of(b * KBLK, KBLK), KBLK)
            scores = contract_cols(k_all[at, :], queries)
            allowed = tile_lanes(segk_ref[at, :], 2 * QBLK // 128) == seg_q
            scores = jnp.where(allowed, scores, SCORE_MASK)
            new_largest = jnp.maximum(largest, jnp.max(scores, axis=0, keepdims=True))
            weights = jnp.exp(scores - new_largest)
            shrink = jnp.exp(largest - new_largest)
            total = total * shrink + jnp.sum(weights, axis=0, keepdims=True)
            low = weights.astype(BF16)
            acc_a = acc_a * shrink[:, :QBLK] + matmul(v_turn[b, :HD, :], low[:, :QBLK])
            acc_b = acc_b * shrink[:, QBLK:] + matmul(v_turn[b, HD:, :], low[:, QBLK:])
            return new_largest, total, acc_a, acc_b

        start = (
            jnp.full((1, 2 * QBLK), SCORE_MASK, F32),
            jnp.zeros((1, 2 * QBLK), F32),
            jnp.zeros((HD, QBLK), F32),
            jnp.zeros((HD, QBLK), F32),
        )
        largest, total, acc_a, acc_b = lax.fori_loop(0, table[i, 0], step, start)
        inverse = 1.0 / total
        context = jnp.concatenate([acc_a * inverse[:, :QBLK], acc_b * inverse[:, QBLK:]], 0)
        ctx_ref[rows, :] = context.T.astype(BF16)
        lse = largest + jnp.log(total)
        lse_ref[0, 0:1, rows] = lse[:, :QBLK]
        lse_ref[0, 1:2, rows] = lse[:, QBLK:]


def attn_backward_kernel(
    table,
    q_ref,
    k_ref,
    v_ref,
    kh_ref,
    vh_ref,
    segq_ref,
    segk_ref,
    grad_ref,
    ctx_ref,
    lse_ref,
    dq_ref,
    dk_ref,
    dv_ref,
    dh_ref,
    k_all,
    v_all,
    k_turn,
    dk_all,
    dv_all,
):
    own = k_ref.shape[0]
    halo = kh_ref.shape[0]
    k_all[:own, :] = k_ref[...]
    k_all[own:, :] = kh_ref[...]
    v_all[:own, :] = v_ref[...]
    v_all[own:, :] = vh_ref[...]
    for b in range((own + halo) // KBLK):
        k_turn[b] = k_all[b * KBLK : (b + 1) * KBLK, :].T
    dk_all[...] = jnp.zeros_like(dk_all)
    dv_all[...] = jnp.zeros_like(dv_all)
    for i in range(own // QBLK):
        rows = slice(i * QBLK, (i + 1) * QBLK)
        queries = split_pair(q_ref[rows, :] * BF16(HD**-0.5))
        grads = split_pair(grad_ref[rows, :])
        seg_q = tile_lanes(segq_ref[:, rows], 2)
        turned = (grad_ref[rows, :].astype(F32) * ctx_ref[rows, :].astype(F32)).T
        centre = jnp.concatenate(
            [
                jnp.sum(turned[:HD], axis=0, keepdims=True),
                jnp.sum(turned[HD:], axis=0, keepdims=True),
            ],
            1,
        )
        lse = jnp.concatenate([lse_ref[0, 0:1, rows], lse_ref[0, 1:2, rows]], 1)

        def step(j, carry):
            acc_a, acc_b = carry
            b = table[i, j + 1]
            at = pl.ds(pl.multiple_of(b * KBLK, KBLK), KBLK)
            scores = contract_cols(k_all[at, :], queries)
            allowed = tile_lanes(segk_ref[at, :], 2 * QBLK // 128) == seg_q
            probs = jnp.exp(jnp.where(allowed, scores - lse, SCORE_MASK))
            prob_grad = contract_cols(v_all[at, :], grads)
            score_grad = (probs * (prob_grad - centre)).astype(BF16)
            dv_all[at, :] += matmul(probs.astype(BF16), grads)
            dk_all[at, :] += matmul(score_grad, queries)
            acc_a = acc_a + matmul(k_turn[b, :HD, :], score_grad[:, :QBLK])
            acc_b = acc_b + matmul(k_turn[b, HD:, :], score_grad[:, QBLK:])
            return acc_a, acc_b

        start = (jnp.zeros((HD, QBLK), F32), jnp.zeros((HD, QBLK), F32))
        acc_a, acc_b = lax.fori_loop(0, table[i, 0], step, start)
        dq_ref[rows, :] = (jnp.concatenate([acc_a, acc_b], 0) * HD**-0.5).T.astype(BF16)
    dk_ref[...] = dk_all[:own, :].astype(BF16)
    dv_ref[...] = dv_all[:own, :].astype(BF16)
    dh_ref[0] = dk_all[own:, :].astype(BF16)
    dh_ref[1] = dv_all[own:, :].astype(BF16)


def block_table(seg_own, seg_halo):
    first = seg_own[::QBLK][:, None]
    last = seg_own[QBLK - 1 :: QBLK][:, None]

    def bounds(segments):
        below = jnp.sum((segments[None, :] < first).astype(jnp.int32), axis=1)
        upto = jnp.sum((segments[None, :] <= last).astype(jnp.int32), axis=1)
        return below // KBLK, (upto + KBLK - 1) // KBLK

    low, high = bounds(seg_own)
    halo_low, halo_high = bounds(seg_halo)
    own_count = high - low
    count = own_count + halo_high - halo_low
    index = jnp.arange((seg_own.shape[0] + seg_halo.shape[0]) // KBLK, dtype=jnp.int32)[None, :]
    own_blocks = seg_own.shape[0] // KBLK
    blocks = jnp.where(
        index < own_count[:, None],
        low[:, None] + index,
        own_blocks + halo_low[:, None] + index - own_count[:, None],
    )
    return jnp.concatenate([count[:, None], blocks], 1)


def attention_specs(own, halo, pairs):
    def column(length, start):
        return pl.BlockSpec((length, PAIR), lambda p, t: (0, start + p))

    def whole(shape):
        return pl.BlockSpec(shape, lambda p, t: (0,) * len(shape))

    return [
        column(own, 0),
        column(own, pairs),
        column(own, 2 * pairs),
        column(halo, 0),
        column(halo, pairs),
        whole((1, own)),
        whole((own + halo, 128)),
    ], column


def attention_forward(table, qkv, halo_kv, seg_row, seg_keys):
    own, width = qkv.shape[0], qkv.shape[1] // 3
    halo = halo_kv.shape[0]
    pairs = width // PAIR
    specs, column = attention_specs(own, halo, pairs)
    return pl.pallas_call(
        attn_forward_kernel,
        grid_spec=pltpu.PrefetchScalarGridSpec(
            num_scalar_prefetch=1,
            grid=(pairs,),
            in_specs=specs,
            out_specs=[column(own, 0), pl.BlockSpec((1, 2, own), lambda p, t: (p, 0, 0))],
            scratch_shapes=[
                pltpu.VMEM((own + halo, PAIR), BF16),
                pltpu.VMEM(((own + halo) // KBLK, PAIR, KBLK), BF16),
            ],
        ),
        out_shape=[
            jax.ShapeDtypeStruct((own, width), BF16),
            jax.ShapeDtypeStruct((pairs, 2, own), F32),
        ],
        name="attn_forward",
    )(table, qkv, qkv, qkv, halo_kv, halo_kv, seg_row, seg_keys)


def attention_backward(table, qkv, halo_kv, seg_row, seg_keys, grad, context, lse):
    own, width = qkv.shape[0], qkv.shape[1] // 3
    halo = halo_kv.shape[0]
    pairs = width // PAIR
    specs, column = attention_specs(own, halo, pairs)
    low = jax.ShapeDtypeStruct((own, width), BF16)
    return pl.pallas_call(
        attn_backward_kernel,
        grid_spec=pltpu.PrefetchScalarGridSpec(
            num_scalar_prefetch=1,
            grid=(pairs,),
            in_specs=specs
            + [column(own, 0), column(own, 0), pl.BlockSpec((1, 2, own), lambda p, t: (p, 0, 0))],
            out_specs=[column(own, 0)] * 3
            + [pl.BlockSpec((2, halo, PAIR), lambda p, t: (0, 0, p))],
            scratch_shapes=[
                pltpu.VMEM((own + halo, PAIR), BF16),
                pltpu.VMEM((own + halo, PAIR), BF16),
                pltpu.VMEM(((own + halo) // KBLK, PAIR, KBLK), BF16),
                pltpu.VMEM((own + halo, PAIR), F32),
                pltpu.VMEM((own + halo, PAIR), F32),
            ],
        ),
        out_shape=[low, low, low, jax.ShapeDtypeStruct((2, halo, width), BF16)],
        name="attn_backward",
    )(table, qkv, qkv, qkv, halo_kv, halo_kv, seg_row, seg_keys, grad, context, lse)


def adamw(master, gradient, first, second, rate, decay):
    first_new = BETA_FIRST * first + (1.0 - BETA_FIRST) * gradient
    second_new = BETA_SECOND * second + (1.0 - BETA_SECOND) * gradient * gradient
    first_hat = first_new / (1.0 - BETA_FIRST**STEP)
    second_hat = second_new / (1.0 - BETA_SECOND**STEP)
    master_new = master - rate * (first_hat / (jnp.sqrt(second_hat) + ADAM_EPS) + decay * master)
    return (master_new, first_new, second_new)


BOTH = ("rows", "genes")
SWAP = [(0, 1), (1, 0)]


def gather_rows(shard):
    return lax.all_gather(shard, BOTH, axis=0, tiled=True)


def scatter_rows(whole):
    return lax.psum_scatter(whole, BOTH, scatter_dimension=0, tiled=True).astype(F32)


def on_device(
    tokens, segment_ids, cotangent, matrices, vectors, mat_first, mat_second, vec_first, vec_second
):
    row_count, own, width = tokens.shape
    hidden = matrices.shape[2]
    vec_rows = vectors.shape[0]
    halo = min(CELL_MAX, own)
    core = lax.axis_index("genes")
    mat_low = matrices.astype(BF16)
    vec_low = jnp.pad(vectors.astype(BF16).T, ((0, 0), (0, VEC_COLS - vec_rows)))
    first_part = gather_rows(jnp.concatenate([mat_low[0, :, : 3 * width], vec_low], 1))
    second_part = gather_rows(
        jnp.concatenate([mat_low[1], mat_low[2], mat_low[0, :, 3 * width :]], 1)
    )
    w_qkv = first_part[:, : 3 * width]
    vec = first_part[:, 3 * width : 3 * width + vec_rows].T.astype(F32)
    w_up = second_part[:, :hidden]
    w_down = second_part[:, hidden : 2 * hidden]
    w_out = second_part[:, 2 * hidden :]

    x = tokens.reshape(own, width).astype(F32)
    hat_one, factor_one = norm_stats(x)
    n1 = (hat_one * vec[0] + vec[1]).astype(BF16)
    qkv_bias = jnp.concatenate([vec[2], jnp.zeros((width,), F32), vec[3]])
    qkv = (matmul(n1, w_qkv) + qkv_bias).astype(BF16)

    segments = segment_ids.reshape(-1)
    seg_own = lax.dynamic_slice_in_dim(segments, core * own, own)
    halo_start = jnp.where(core == 0, own, own - halo)
    seg_halo = lax.dynamic_slice_in_dim(segments, halo_start, halo)
    table = block_table(seg_own, seg_halo)
    seg_row = seg_own[None, :]
    seg_keys = jnp.broadcast_to(jnp.concatenate([seg_own, seg_halo])[:, None], (own + halo, 128))
    send_start = jnp.where(core == 0, own - halo, 0)
    halo_kv = lax.ppermute(
        lax.dynamic_slice(qkv, (send_start, width), (halo, 2 * width)), "genes", SWAP
    )
    ctx, lse = attention_forward(table, qkv, halo_kv, seg_row, seg_keys)

    x2 = x + matmul(ctx, w_out) + vec[4]
    hat_two, factor_two = norm_stats(x2)
    n2 = (hat_two * vec[5] + vec[6]).astype(BF16)
    u = matmul(n2, w_up) + vec[7:11].reshape(hidden)
    cdf, bell = normal_parts(u)
    act = (u * cdf).astype(BF16)
    slope = cdf + u * bell
    layer_out = (x2 + contract_cols(act, w_down) + vec[11]).astype(BF16)

    dy_low = cotangent.reshape(own, width)
    dy = dy_low.astype(F32)
    g_down = contract_rows(dy_low, act).astype(BF16)
    gb_down = jnp.sum(dy, axis=0)
    du = (slope * matmul(dy_low, w_down)).astype(BF16)
    gb_up = jnp.sum(du.astype(F32), axis=0)
    g_up = contract_rows(n2, du).astype(BF16)
    ffn_shard = scatter_rows(jnp.concatenate([g_up, g_down], 1))
    dn2 = contract_cols(du, w_up)
    dx2 = dy + norm_back(dn2, hat_two, factor_two, vec[5])
    g_gain_two = jnp.sum(dn2 * hat_two, axis=0)
    g_shift_two = jnp.sum(dn2, axis=0)
    da = dx2.astype(BF16)
    gb_out = jnp.sum(da.astype(F32), axis=0)
    dctx = contract_cols(da, w_out).astype(BF16)
    g_out = contract_rows(ctx, da).astype(BF16)

    dq, dk, dv, dh = attention_backward(table, qkv, halo_kv, seg_row, seg_keys, dctx, ctx, lse)
    dh = lax.ppermute(dh, "genes", SWAP)
    put = jnp.where(core == 0, own - halo, 0)

    def add_halo(mine, other):
        spread = lax.dynamic_update_slice(jnp.zeros_like(mine), other, (put, 0))
        return (mine.astype(F32) + spread.astype(F32)).astype(BF16)

    dk = add_halo(dk, dh[0])
    dv = add_halo(dv, dh[1])
    dqkv = jnp.concatenate([dq, dk, dv], 1)
    g_qkv = contract_rows(n1, dqkv).astype(BF16)
    dn1 = contract_cols(dqkv, w_qkv)
    gb_query = jnp.sum(dq.astype(F32), axis=0)
    gb_value = jnp.sum(dv.astype(F32), axis=0)
    g_gain_one = jnp.sum(dn1 * hat_one, axis=0)
    g_shift_one = jnp.sum(dn1, axis=0)
    tokens_grad = (dx2 + norm_back(dn1, hat_one, factor_one, vec[0])).reshape(row_count, own, width)
    g_vec = jnp.concatenate(
        [
            jnp.stack(
                [g_gain_one, g_shift_one, gb_query, gb_value, gb_out, g_gain_two, g_shift_two]
            ),
            gb_up.reshape(hidden // width, width),
            gb_down[None],
        ],
        0,
    )
    g_vec = jnp.pad(g_vec.T.astype(BF16), ((0, 0), (0, VEC_COLS - vec_rows)))
    attn_shard = scatter_rows(jnp.concatenate([g_qkv, g_out, g_vec], 1))
    mat_shard = jnp.stack([attn_shard[:, : 4 * width], ffn_shard[:, :hidden], ffn_shard[:, hidden:]])
    vec_shard = attn_shard[:, 4 * width : 4 * width + vec_rows].T
    matrices_out = adamw(matrices, mat_shard, mat_first, mat_second, MATRIX_RATE, MATRIX_DECAY)
    vectors_out = adamw(vectors, vec_shard, vec_first, vec_second, VECTOR_RATE, 0.0)
    return (layer_out.reshape(row_count, own, width), tokens_grad) + matrices_out + vectors_out


def solution(mesh):
    tokens_spec = P("rows", "genes", None)
    mat_spec = P(None, ("rows", "genes"), None)
    vec_spec = P(None, ("rows", "genes"))
    in_specs = (
        tokens_spec,
        P("rows", None),
        tokens_spec,
        mat_spec,
        vec_spec,
        mat_spec,
        mat_spec,
        vec_spec,
        vec_spec,
    )
    out_specs = (tokens_spec,) * 2 + (mat_spec,) * 3 + (vec_spec,) * 3
    return jax.shard_map(
        on_device, mesh=mesh, in_specs=in_specs, out_specs=out_specs, check_vma=False
    )
```

```python
import jax
import jax.numpy as jnp
from jax import lax
from jax.experimental import pallas as pl
from jax.experimental.pallas import tpu as pltpu
from jax.sharding import PartitionSpec as P

HD = 64
STEP = 10
CELL_MAX = 512

BETA_FIRST = 0.5
BETA_SECOND = 0.5
ADAM_EPS = 1e-08
MATRIX_RATE = 0.05
VECTOR_RATE = 0.3
MATRIX_DECAY = 0.01
NORM_EPS = 1e-05
SCORE_MASK = -1e30
PAIR = 2 * HD
QBLK = 256
KBLK = 256
VEC_COLS = 128

F32 = jnp.float32
BF16 = jnp.bfloat16


def contract_rows(former, latter):
    return lax.dot_general(
        former, latter, (((0,), (0,)), ((), ())), preferred_element_type=jnp.float32
    )


def contract_cols(former, latter):
    return lax.dot_general(
        former, latter, (((1,), (1,)), ((), ())), preferred_element_type=jnp.float32
    )


def matmul(former, latter):
    return lax.dot_general(
        former, latter, (((1,), (0,)), ((), ())), preferred_element_type=jnp.float32
    )


def norm_stats(values):
    centre = values - jnp.mean(values, axis=-1, keepdims=True)
    spread = jnp.mean(centre * centre, axis=-1, keepdims=True)
    factor = lax.rsqrt(spread + NORM_EPS)
    return centre * factor, factor


def norm_back(grad, hat, factor, gain):
    scaled = grad * gain
    mean_one = jnp.mean(scaled, axis=-1, keepdims=True)
    mean_two = jnp.mean(scaled * hat, axis=-1, keepdims=True)
    return factor * (scaled - mean_one - hat * mean_two)


def normal_parts(values):
    bell = jnp.exp(-0.5 * values * values)
    t = 1.0 / (1.0 + 0.3275911 * 0.7071067811865476 * jnp.abs(values))
    poly = t * (
        0.254829592
        + t * (-0.284496736 + t * (1.421413741 + t * (-1.453152027 + t * 1.061405429)))
    )
    tail = 0.5 * poly * bell
    return jnp.where(values < 0.0, tail, 1.0 - tail), 0.3989422804014327 * bell


def split_pair(block):
    lane = lax.broadcasted_iota(jnp.int32, block.shape, 1)
    zero = jnp.zeros_like(block)
    return jnp.concatenate(
        [jnp.where(lane < HD, block, zero), jnp.where(lane < HD, zero, block)], 0
    )


def tile_lanes(block, times):
    return jnp.concatenate([block] * times, 1)


def attn_forward_kernel(
    table, q_ref, k_ref, v_ref, kh_ref, vh_ref, segq_ref, segk_ref, ctx_ref, lse_ref, k_all, v_turn
):
    own = k_ref.shape[0]
    halo = kh_ref.shape[0]
    k_all[:own, :] = k_ref[...]
    k_all[own:, :] = kh_ref[...]
    for b in range(own // KBLK):
        v_turn[b] = v_ref[b * KBLK : (b + 1) * KBLK, :].T
    for b in range(halo // KBLK):
        v_turn[own // KBLK + b] = vh_ref[b * KBLK : (b + 1) * KBLK, :].T
    for i in range(own // QBLK):
        rows = slice(i * QBLK, (i + 1) * QBLK)
        queries = split_pair(q_ref[rows, :] * BF16(HD**-0.5))
        seg_q = tile_lanes(segq_ref[:, rows], 2)

        def step(j, carry):
            largest, total, acc_a, acc_b = carry
            b = table[i, j + 1]
            at = pl.ds(pl.multiple_of(b * KBLK, KBLK), KBLK)
            scores = contract_cols(k_all[at, :], queries)
            allowed = tile_lanes(segk_ref[at, :], 2 * QBLK // 128) == seg_q
            scores = jnp.where(allowed, scores, SCORE_MASK)
            new_largest = jnp.maximum(largest, jnp.max(scores, axis=0, keepdims=True))
            weights = jnp.exp(scores - new_largest)
            shrink = jnp.exp(largest - new_largest)
            total = total * shrink + jnp.sum(weights, axis=0, keepdims=True)
            low = weights.astype(BF16)
            acc_a = acc_a * shrink[:, :QBLK] + matmul(v_turn[b, :HD, :], low[:, :QBLK])
            acc_b = acc_b * shrink[:, QBLK:] + matmul(v_turn[b, HD:, :], low[:, QBLK:])
            return new_largest, total, acc_a, acc_b

        start = (
            jnp.full((1, 2 * QBLK), SCORE_MASK, F32),
            jnp.zeros((1, 2 * QBLK), F32),
            jnp.zeros((HD, QBLK), F32),
            jnp.zeros((HD, QBLK), F32),
        )
        largest, total, acc_a, acc_b = lax.fori_loop(0, table[i, 0], step, start)
        inverse = 1.0 / total
        context = jnp.concatenate([acc_a * inverse[:, :QBLK], acc_b * inverse[:, QBLK:]], 0)
        ctx_ref[rows, :] = context.T.astype(BF16)
        lse = largest + jnp.log(total)
        lse_ref[0, 0:1, rows] = lse[:, :QBLK]
        lse_ref[0, 1:2, rows] = lse[:, QBLK:]


def attn_backward_kernel(
    table,
    q_ref,
    k_ref,
    v_ref,
    kh_ref,
    vh_ref,
    segq_ref,
    segk_ref,
    grad_ref,
    ctx_ref,
    lse_ref,
    dq_ref,
    dk_ref,
    dv_ref,
    dh_ref,
    k_all,
    v_all,
    k_turn,
    dk_all,
    dv_all,
):
    own = k_ref.shape[0]
    halo = kh_ref.shape[0]
    k_all[:own, :] = k_ref[...]
    k_all[own:, :] = kh_ref[...]
    v_all[:own, :] = v_ref[...]
    v_all[own:, :] = vh_ref[...]
    for b in range((own + halo) // KBLK):
        k_turn[b] = k_all[b * KBLK : (b + 1) * KBLK, :].T
    dk_all[...] = jnp.zeros_like(dk_all)
    dv_all[...] = jnp.zeros_like(dv_all)
    for i in range(own // QBLK):
        rows = slice(i * QBLK, (i + 1) * QBLK)
        queries = split_pair(q_ref[rows, :] * BF16(HD**-0.5))
        grads = split_pair(grad_ref[rows, :])
        seg_q = tile_lanes(segq_ref[:, rows], 2)
        turned = (grad_ref[rows, :].astype(F32) * ctx_ref[rows, :].astype(F32)).T
        centre = jnp.concatenate(
            [
                jnp.sum(turned[:HD], axis=0, keepdims=True),
                jnp.sum(turned[HD:], axis=0, keepdims=True),
            ],
            1,
        )
        lse = jnp.concatenate([lse_ref[0, 0:1, rows], lse_ref[0, 1:2, rows]], 1)

        def step(j, carry):
            acc_a, acc_b = carry
            b = table[i, j + 1]
            at = pl.ds(pl.multiple_of(b * KBLK, KBLK), KBLK)
            scores = contract_cols(k_all[at, :], queries)
            allowed = tile_lanes(segk_ref[at, :], 2 * QBLK // 128) == seg_q
            probs = jnp.exp(jnp.where(allowed, scores - lse, SCORE_MASK))
            prob_grad = contract_cols(v_all[at, :], grads)
            score_grad = (probs * (prob_grad - centre)).astype(BF16)
            dv_all[at, :] += matmul(probs.astype(BF16), grads)
            dk_all[at, :] += matmul(score_grad, queries)
            acc_a = acc_a + matmul(k_turn[b, :HD, :], score_grad[:, :QBLK])
            acc_b = acc_b + matmul(k_turn[b, HD:, :], score_grad[:, QBLK:])
            return acc_a, acc_b

        start = (jnp.zeros((HD, QBLK), F32), jnp.zeros((HD, QBLK), F32))
        acc_a, acc_b = lax.fori_loop(0, table[i, 0], step, start)
        dq_ref[rows, :] = (jnp.concatenate([acc_a, acc_b], 0) * HD**-0.5).T.astype(BF16)
    dk_ref[...] = dk_all[:own, :].astype(BF16)
    dv_ref[...] = dv_all[:own, :].astype(BF16)
    dh_ref[0] = dk_all[own:, :].astype(BF16)
    dh_ref[1] = dv_all[own:, :].astype(BF16)


def block_table(seg_own, seg_halo):
    first = seg_own[::QBLK][:, None]
    last = seg_own[QBLK - 1 :: QBLK][:, None]

    def bounds(segments):
        below = jnp.sum((segments[None, :] < first).astype(jnp.int32), axis=1)
        upto = jnp.sum((segments[None, :] <= last).astype(jnp.int32), axis=1)
        return below // KBLK, (upto + KBLK - 1) // KBLK

    low, high = bounds(seg_own)
    halo_low, halo_high = bounds(seg_halo)
    own_count = high - low
    count = own_count + halo_high - halo_low
    index = jnp.arange((seg_own.shape[0] + seg_halo.shape[0]) // KBLK, dtype=jnp.int32)[None, :]
    own_blocks = seg_own.shape[0] // KBLK
    blocks = jnp.where(
        index < own_count[:, None],
        low[:, None] + index,
        own_blocks + halo_low[:, None] + index - own_count[:, None],
    )
    return jnp.concatenate([count[:, None], blocks], 1)


def attention_specs(own, halo, pairs):
    def column(length, start):
        return pl.BlockSpec((length, PAIR), lambda p, t: (0, start + p))

    def whole(shape):
        return pl.BlockSpec(shape, lambda p, t: (0,) * len(shape))

    return [
        column(own, 0),
        column(own, pairs),
        column(own, 2 * pairs),
        column(halo, 0),
        column(halo, pairs),
        whole((1, own)),
        whole((own + halo, 128)),
    ], column


def attention_forward(table, qkv, halo_kv, seg_row, seg_keys):
    own, width = qkv.shape[0], qkv.shape[1] // 3
    halo = halo_kv.shape[0]
    pairs = width // PAIR
    specs, column = attention_specs(own, halo, pairs)
    return pl.pallas_call(
        attn_forward_kernel,
        grid_spec=pltpu.PrefetchScalarGridSpec(
            num_scalar_prefetch=1,
            grid=(pairs,),
            in_specs=specs,
            out_specs=[column(own, 0), pl.BlockSpec((1, 2, own), lambda p, t: (p, 0, 0))],
            scratch_shapes=[
                pltpu.VMEM((own + halo, PAIR), BF16),
                pltpu.VMEM(((own + halo) // KBLK, PAIR, KBLK), BF16),
            ],
        ),
        out_shape=[
            jax.ShapeDtypeStruct((own, width), BF16),
            jax.ShapeDtypeStruct((pairs, 2, own), F32),
        ],
        name="attn_forward",
    )(table, qkv, qkv, qkv, halo_kv, halo_kv, seg_row, seg_keys)


def attention_backward(table, qkv, halo_kv, seg_row, seg_keys, grad, context, lse):
    own, width = qkv.shape[0], qkv.shape[1] // 3
    halo = halo_kv.shape[0]
    pairs = width // PAIR
    specs, column = attention_specs(own, halo, pairs)
    low = jax.ShapeDtypeStruct((own, width), BF16)
    return pl.pallas_call(
        attn_backward_kernel,
        grid_spec=pltpu.PrefetchScalarGridSpec(
            num_scalar_prefetch=1,
            grid=(pairs,),
            in_specs=specs
            + [column(own, 0), column(own, 0), pl.BlockSpec((1, 2, own), lambda p, t: (p, 0, 0))],
            out_specs=[column(own, 0)] * 3
            + [pl.BlockSpec((2, halo, PAIR), lambda p, t: (0, 0, p))],
            scratch_shapes=[
                pltpu.VMEM((own + halo, PAIR), BF16),
                pltpu.VMEM((own + halo, PAIR), BF16),
                pltpu.VMEM(((own + halo) // KBLK, PAIR, KBLK), BF16),
                pltpu.VMEM((own + halo, PAIR), F32),
                pltpu.VMEM((own + halo, PAIR), F32),
            ],
        ),
        out_shape=[low, low, low, jax.ShapeDtypeStruct((2, halo, width), BF16)],
        name="attn_backward",
    )(table, qkv, qkv, qkv, halo_kv, halo_kv, seg_row, seg_keys, grad, context, lse)


def adamw(master, gradient, first, second, rate, decay):
    first_new = BETA_FIRST * first + (1.0 - BETA_FIRST) * gradient
    second_new = BETA_SECOND * second + (1.0 - BETA_SECOND) * gradient * gradient
    first_hat = first_new / (1.0 - BETA_FIRST**STEP)
    second_hat = second_new / (1.0 - BETA_SECOND**STEP)
    master_new = master - rate * (first_hat / (jnp.sqrt(second_hat) + ADAM_EPS) + decay * master)
    return (master_new, first_new, second_new)


BOTH = ("rows", "genes")
SWAP = [(0, 1), (1, 0)]
PLANE = 4


def swap_rows(block, distance):
    count = lax.axis_size("rows")
    return lax.ppermute(block, "rows", [(i, i ^ distance) for i in range(count)])


def gather_late(shard):
    return lax.all_gather(shard, BOTH, axis=0, tiled=True)


def gather_soon(shard):
    height, cols = shard.shape
    count = lax.axis_size("rows")
    me = lax.axis_index("rows")
    core = lax.axis_index("genes")
    groups = count // PLANE
    column = jnp.zeros((groups, height, cols), shard.dtype)
    for d in range(groups):
        piece = swap_rows(shard, PLANE * d) if d else shard
        column = lax.dynamic_update_slice(column, piece[None], ((me // PLANE) ^ d, 0, 0))
    grid = jnp.zeros((groups, PLANE, height, cols), shard.dtype)
    for d in range(PLANE):
        piece = swap_rows(column, d) if d else column
        grid = lax.dynamic_update_slice(grid, piece[:, None], (0, (me % PLANE) ^ d, 0, 0))
    grid = grid.reshape(count, height, cols)
    other = lax.ppermute(grid, "genes", SWAP)
    both = jnp.stack([jnp.where(core == 0, grid, other), jnp.where(core == 0, other, grid)], 1)
    return both.reshape(2 * count * height, cols)


def scatter_late(whole):
    return lax.psum_scatter(whole, BOTH, scatter_dimension=0, tiled=True).astype(F32)


def pick(block, index, axis):
    return lax.dynamic_index_in_dim(block, index, axis, keepdims=False)


def scatter_soon(whole):
    count = lax.axis_size("rows")
    me = lax.axis_index("rows")
    core = lax.axis_index("genes")
    groups = count // PLANE
    cols = whole.shape[1]
    halves = whole.reshape(groups, PLANE, 2, -1, cols)
    other = lax.ppermute(pick(halves, 1 - core, 2), "genes", SWAP)
    block = (pick(halves, core, 2).astype(F32) + other.astype(F32)).astype(BF16)
    total = pick(block, me % PLANE, 1).astype(F32)
    for d in range(1, PLANE):
        total = total + swap_rows(pick(block, (me % PLANE) ^ d, 1), d).astype(F32)
    block = total.astype(BF16)
    total = pick(block, me // PLANE, 0).astype(F32)
    for d in range(1, groups):
        total = total + swap_rows(pick(block, (me // PLANE) ^ d, 0), PLANE * d).astype(F32)
    return total


def on_device(
    tokens, segment_ids, cotangent, matrices, vectors, mat_first, mat_second, vec_first, vec_second
):
    row_count, own, width = tokens.shape
    hidden = matrices.shape[2]
    vec_rows = vectors.shape[0]
    halo = min(CELL_MAX, own)
    core = lax.axis_index("genes")
    mat_low = matrices.astype(BF16)
    vec_low = jnp.pad(vectors.astype(BF16).T, ((0, 0), (0, VEC_COLS - vec_rows)))
    first_part = gather_soon(jnp.concatenate([mat_low[0, :, : 3 * width], vec_low], 1))
    second_part = gather_late(
        jnp.concatenate([mat_low[1], mat_low[2], mat_low[0, :, 3 * width :]], 1)
    )
    w_qkv = first_part[:, : 3 * width]
    vec = first_part[:, 3 * width : 3 * width + vec_rows].T.astype(F32)
    w_up = second_part[:, :hidden]
    w_down = second_part[:, hidden : 2 * hidden]
    w_out = second_part[:, 2 * hidden :]

    x = tokens.reshape(own, width).astype(F32)
    hat_one, factor_one = norm_stats(x)
    n1 = (hat_one * vec[0] + vec[1]).astype(BF16)
    qkv_bias = jnp.concatenate([vec[2], jnp.zeros((width,), F32), vec[3]])
    qkv = (matmul(n1, w_qkv) + qkv_bias).astype(BF16)

    segments = segment_ids.reshape(-1)
    seg_own = lax.dynamic_slice_in_dim(segments, core * own, own)
    halo_start = jnp.where(core == 0, own, own - halo)
    seg_halo = lax.dynamic_slice_in_dim(segments, halo_start, halo)
    table = block_table(seg_own, seg_halo)
    seg_row = seg_own[None, :]
    seg_keys = jnp.broadcast_to(jnp.concatenate([seg_own, seg_halo])[:, None], (own + halo, 128))
    send_start = jnp.where(core == 0, own - halo, 0)
    halo_kv = lax.ppermute(
        lax.dynamic_slice(qkv, (send_start, width), (halo, 2 * width)), "genes", SWAP
    )
    ctx, lse = attention_forward(table, qkv, halo_kv, seg_row, seg_keys)

    x2 = x + matmul(ctx, w_out) + vec[4]
    hat_two, factor_two = norm_stats(x2)
    n2 = (hat_two * vec[5] + vec[6]).astype(BF16)
    u = matmul(n2, w_up) + vec[7:11].reshape(hidden)
    cdf, bell = normal_parts(u)
    act = (u * cdf).astype(BF16)
    slope = cdf + u * bell
    layer_out = (x2 + contract_cols(act, w_down) + vec[11]).astype(BF16)

    dy_low = cotangent.reshape(own, width)
    dy = dy_low.astype(F32)
    g_down = contract_rows(dy_low, act).astype(BF16)
    gb_down = jnp.sum(dy, axis=0)
    du = (slope * matmul(dy_low, w_down)).astype(BF16)
    gb_up = jnp.sum(du.astype(F32), axis=0)
    g_up = contract_rows(n2, du).astype(BF16)
    dn2 = contract_cols(du, w_up)
    dx2 = dy + norm_back(dn2, hat_two, factor_two, vec[5])
    g_gain_two = jnp.sum(dn2 * hat_two, axis=0)
    g_shift_two = jnp.sum(dn2, axis=0)
    da = dx2.astype(BF16)
    gb_out = jnp.sum(da.astype(F32), axis=0)
    dctx = contract_cols(da, w_out).astype(BF16)
    g_out = contract_rows(ctx, da).astype(BF16)
    early, dctx = lax.optimization_barrier((jnp.concatenate([g_up, g_down, g_out], 1), dctx))
    early_shard = scatter_late(early)

    dq, dk, dv, dh = attention_backward(table, qkv, halo_kv, seg_row, seg_keys, dctx, ctx, lse)
    dh = lax.ppermute(dh, "genes", SWAP)
    put = jnp.where(core == 0, own - halo, 0)

    def add_halo(mine, other):
        spread = lax.dynamic_update_slice(jnp.zeros_like(mine), other, (put, 0))
        return (mine.astype(F32) + spread.astype(F32)).astype(BF16)

    dk = add_halo(dk, dh[0])
    dv = add_halo(dv, dh[1])
    dqkv = jnp.concatenate([dq, dk, dv], 1)
    g_qkv = contract_rows(n1, dqkv).astype(BF16)
    qkv_shard = scatter_soon(g_qkv)
    dn1 = contract_cols(dqkv, w_qkv)
    gb_query = jnp.sum(dq.astype(F32), axis=0)
    gb_value = jnp.sum(dv.astype(F32), axis=0)
    g_gain_one = jnp.sum(dn1 * hat_one, axis=0)
    g_shift_one = jnp.sum(dn1, axis=0)
    tokens_grad = (dx2 + norm_back(dn1, hat_one, factor_one, vec[0])).reshape(row_count, own, width)
    g_vec = jnp.concatenate(
        [
            jnp.stack(
                [g_gain_one, g_shift_one, gb_query, gb_value, gb_out, g_gain_two, g_shift_two]
            ),
            gb_up.reshape(hidden // width, width),
            gb_down[None],
        ],
        0,
    )
    g_vec = jnp.pad(g_vec.T.astype(BF16), ((0, 0), (0, VEC_COLS - vec_rows)))
    vec_shard = scatter_soon(g_vec)[:, :vec_rows].T
    mat_shard = jnp.stack(
        [
            jnp.concatenate([qkv_shard, early_shard[:, 2 * hidden :]], 1),
            early_shard[:, :hidden],
            early_shard[:, hidden : 2 * hidden],
        ]
    )
    matrices_out = adamw(matrices, mat_shard, mat_first, mat_second, MATRIX_RATE, MATRIX_DECAY)
    vectors_out = adamw(vectors, vec_shard, vec_first, vec_second, VECTOR_RATE, 0.0)
    return (layer_out.reshape(row_count, own, width), tokens_grad) + matrices_out + vectors_out


def solution(mesh):
    tokens_spec = P("rows", "genes", None)
    mat_spec = P(None, ("rows", "genes"), None)
    vec_spec = P(None, ("rows", "genes"))
    in_specs = (
        tokens_spec,
        P("rows", None),
        tokens_spec,
        mat_spec,
        vec_spec,
        mat_spec,
        mat_spec,
        vec_spec,
        vec_spec,
    )
    out_specs = (tokens_spec,) * 2 + (mat_spec,) * 3 + (vec_spec,) * 3
    return jax.shard_map(
        on_device, mesh=mesh, in_specs=in_specs, out_specs=out_specs, check_vma=False
    )
```
